512 devices in a mesh: dir: 16 (over x, z_hi, core), elem: 32 (over z_lo, y).
Axes of the slice: x: 4, y: 8, z: 8 (z_hi: 2, z_lo: 4; z = z_hi * 4 + z_lo), core: 2. Of those that a mesh axis runs over, the one named last changes fastest.
Arguments:
- panel_angles: float32 [2, 16384], P(None, 'elem'), may hold values from -3.140625 to 3.140625
- impedance: float32 [16384], P('elem'), may hold values from 0.3 to 3
- quad_count: int32 [16384], P('elem'), may hold values from 1 to 4
- receivers: int32 [1024], replicated, may hold values from 0 to 4095
- farfield_data: float32 [2, 256, 1024], P(None, 'dir'), may hold values from -24 to 24
- warm_density: float32 [2, 256, 16384], P(None, 'dir', 'elem'), may hold values from -6 to 6
Outputs:
- gradient: float32 [16384], P('elem')
- density: float32 [2, 256, 16384], P(None, 'dir', 'elem')
The draws below stay inside these ranges and needn't reach their ends.
Inputs may be any that keep to these rules, and one draw needn't show every extreme that they name: Index into a lattice of 4096 directions; receivers may share an index.
All inputs are finite; a program needn't handle non-finite values.
Results may differ from the reference program's by a relative error of at most 0.0038.
Values may be sent and summed in bfloat16 or wider, within the bound.
No kernel may reach another device: no remote copies, remote signals or barrier semaphores. Data moves between devices by JAX's collectives and lax.ppermute only.
A program may use at most 128 MiB of HBM per device.

```python
import math
import jax
import jax.numpy as jnp
from jax import lax

PANELS = 16384
RECV = 1024
ITERS = 1
RBANK = 4096
NDIR = 256


def draw_farfield_data(key, part):
    keys = jax.random.split(jax.random.fold_in(key, 7177), 1)
    values = 3.0 * jax.random.normal(keys[0], (2, NDIR, RECV), jnp.float32)
    return jnp.clip(values, -24.0, 24.0)


def touch_ends(entries, own_key, low, top_value):
    index_at = [jax.random.randint(jax.random.fold_in(own_key, axis), (), 0, length) for axis, length in enumerate(entries.shape)]
    widest = entries.shape.index(max(entries.shape))
    next_to = index_at[:widest] + [(index_at[widest] + 1) % entries.shape[widest]] + index_at[widest + 1:]
    return entries.at[tuple(index_at)].set(low).at[tuple(next_to)].set(top_value)


def level_of(rng, shape, pieces, least, largest):
    factor_of = 1.0
    for dim, blocks in pieces:
        draws = jax.random.uniform(jax.random.fold_in(jax.random.fold_in(rng, 6), dim), (blocks,), jnp.float32, least / len(pieces), largest / len(pieces))
        factor_of = factor_of * jnp.repeat(jnp.exp(draws), shape[dim] // blocks).reshape((-1,) + (1,) * (len(shape) - 1 - dim))
    return factor_of


def bell_draw(key, extent, scale, most, cuts=(), held_as=jnp.bfloat16):
    factor_of = level_of(key, extent, cuts, -0.22, 0.18) if cuts else 1.0
    drawn = jax.random.normal(key, extent, jnp.float32) * scale * factor_of
    return jnp.minimum(jnp.maximum(drawn, -most), most).astype(held_as)


def setup_inputs(seed: int = 0) -> dict:
    arg_keys = jax.random.split(jax.random.key(seed), 7)
    return {
        "panel_angles": jnp.clip(jax.random.uniform(arg_keys[0], (2, PANELS), jnp.float32, -3.140625, 3.140625), -3.140625, 3.140625),
        "impedance": jnp.clip(jnp.exp(math.log(3.0) - 2.3025851 * jax.random.uniform(arg_keys[1], (PANELS,), jnp.float32) ** level_of(arg_keys[1], (PANELS,), ((0, 32),), -0.2, 0.2)), 0.3, 3.0),
        "quad_count": touch_ends(jax.random.randint(arg_keys[2], (PANELS,), 1, 5), jax.random.fold_in(arg_keys[2], 1), 1, 4).astype(jnp.int32),
        "receivers": touch_ends(jax.random.randint(arg_keys[3], (RECV,), 0, RBANK), jax.random.fold_in(arg_keys[3], 1), 0, RBANK - 1).astype(jnp.int32),
        "farfield_data": draw_farfield_data(jax.random.fold_in(arg_keys[6], 71), 0),
        "warm_density": bell_draw(arg_keys[5], (2, NDIR, PANELS), 1.0, 6.0, ((1, 16), (2, 32)), jnp.float32),
    }


WAVENUM = 32.0
SOFTEN = 0.0025
tile_rows = 512

def positions(angles):
    phi = angles[0]
    psi = angles[1]
    return jnp.stack([4.0 * jnp.cos(psi), jnp.sin(psi) * jnp.cos(phi), 0.6 * jnp.sin(psi) * jnp.sin(phi)])

def weights(counts):
    return counts.astype(jnp.float32) * (0.5 / (4.0 * math.sqrt(PANELS)))

def lattice(index, count):
    where = index.astype(jnp.float32)
    height = 1.0 - (2.0 * where + 1.0) / count
    radius = jnp.sqrt(1.0 - height * height)
    turn = where * (math.pi * (3.0 - math.sqrt(5.0)))
    return jnp.stack([radius * jnp.cos(turn), radius * jnp.sin(turn), height])

def plane(dvec, pos):
    phase = WAVENUM * lax.optimization_barrier(jnp.sum(dvec[:, :, None] * pos[:, None, :], axis=0))
    return jnp.stack([jnp.cos(phase), jnp.sin(phase)])

def far_table(pos, rdir):
    theta = WAVENUM * lax.optimization_barrier(jnp.sum(pos[:, :, None] * rdir[:, None, :], axis=0))
    return (jnp.cos(theta).astype(jnp.bfloat16), jnp.sin(theta).astype(jnp.bfloat16))

def kernel_tile(src, tgt):
    dist = lax.optimization_barrier(jnp.sum((src[:, :, None] - tgt[:, None, :]) ** 2, axis=0))
    rho = jnp.sqrt(dist + SOFTEN)
    return ((jnp.cos(WAVENUM * rho) / rho).astype(jnp.bfloat16), (jnp.sin(WAVENUM * rho) / rho).astype(jnp.bfloat16))

def apply(vec, cos_t, sin_t, sign, axis):
    half = vec.shape[1]
    stacked = vec.reshape(2 * half, vec.shape[2])
    dims = (((1,), (axis,)), ((), ()))
    first = lax.dot_general(stacked, cos_t, dims, preferred_element_type=jnp.float32)
    second = lax.dot_general(stacked, sin_t, dims, preferred_element_type=jnp.float32)
    real = first[:half] - sign * second[half:]
    imag = first[half:] + sign * second[:half]
    return jnp.stack([real, imag])

def full_apply(vec, pos, sign):
    block = min(tile_rows, PANELS)
    count = PANELS // block
    targets = jnp.transpose(pos.reshape(3, count, block), (1, 0, 2))

    def one(tgt):
        cos_t, sin_t = kernel_tile(pos, tgt)
        return apply(vec, cos_t, sin_t, sign, 0)
    out = lax.map(one, targets)
    return jnp.transpose(out, (1, 2, 0, 3)).reshape(2, vec.shape[1], PANELS)

def reference(panel_angles, impedance, quad_count, receivers, farfield_data, warm_density):
    pos = positions(panel_angles)
    wgt = weights(quad_count)
    wz = wgt * impedance
    ndir = farfield_data.shape[1]
    dvec = lattice(jnp.arange(ndir, dtype=jnp.int32), ndir)
    incident = plane(dvec, pos)
    sigmas = [warm_density]
    state = warm_density
    for step in range(ITERS):
        moved = (wz * state).astype(jnp.bfloat16)
        state = incident - full_apply(moved, pos, 1.0)
        sigmas.append(state)
    rdir = lattice(receivers, RBANK)
    cos_t, sin_t = far_table(pos, rdir)
    farfield = apply((wgt * state).astype(jnp.bfloat16), cos_t, sin_t, -1.0, 0)
    misfit = (farfield - farfield_data).astype(jnp.bfloat16)
    adjoint = wgt * apply(misfit, cos_t, sin_t, 1.0, 1)
    total = jnp.zeros((PANELS,), jnp.float32)
    for step in reversed(range(ITERS)):
        back = -full_apply(adjoint.astype(jnp.bfloat16), pos, -1.0)
        total = total + lax.optimization_barrier(jnp.sum(back * sigmas[step], axis=(0, 1)))
        adjoint = wz * back
    return (total / ndir, state)
```

```python
import math

import jax
import jax.numpy as jnp
from jax import lax
from jax.experimental import pallas as pl
from jax.experimental.pallas import tpu as pltpu
from jax.sharding import PartitionSpec as P

PANELS = 16384
RBANK = 4096
NDIR = 256
WAVENUM = 32.0
SOFTEN = 0.0025
TURNS = WAVENUM / (2.0 * math.pi)

ND = 16
NE = 32
BLOCK = PANELS // NE
SUB = BLOCK // ND
RSUB = 1024 // ND
JD = NDIR // ND
HALF = NE * SUB
QS = 2 * HALF
RH = 1024 // 2
CHUNK = 256
NXC = 8
XC = [[x * 4 + zh * 2 + c for x in range(4) for c in range(2)] for zh in range(2)]

SIN = (6.28318492, -41.34158923, 81.59994333, -76.61447253, 41.34288235, -12.47124353)
COS = (0.99999999, -19.7392045, 64.93911746, -85.45013953, 60.16763095, -25.96759925, 6.52865816)

bf16 = jnp.bfloat16
f32 = jnp.float32


def horner(coef, z):
    acc = coef[-1] * z + coef[-2]
    for c in coef[-3::-1]:
        acc = acc * z + c
    return acc


def circle(turns):
    r = turns - jnp.round(turns)
    z = r * r
    return horner(COS, z), r * horner(SIN, z)


def exchange(x, axis, groups=None):
    return lax.all_to_all(x, axis, 0, 0, axis_index_groups=groups, tiled=True)


def spread(x, count):
    return jnp.broadcast_to(x[None], (count, *x.shape))


def positions(angles):
    phi = angles[0]
    psi = angles[1]
    return jnp.stack(
        [4.0 * jnp.cos(psi), jnp.sin(psi) * jnp.cos(phi), 0.6 * jnp.sin(psi) * jnp.sin(phi)]
    )


def weights(counts):
    return counts.astype(f32) * (0.5 / (4.0 * math.sqrt(PANELS)))


def lattice(index, count):
    where = index.astype(f32)
    height = 1.0 - (2.0 * where + 1.0) / count
    radius = jnp.sqrt(1.0 - height * height)
    turn = where * (math.pi * (3.0 - math.sqrt(5.0)))
    return jnp.stack([radius * jnp.cos(turn), radius * jnp.sin(turn), height])


def nt(a, b):
    return lax.dot_general(a, b, (((1,), (1,)), ((), ())), preferred_element_type=f32)


def tile_body(qrow, qcol, prow, rcol, c_ref, s_ref, b_ref, e_sc, k_sc, acc):
    px, py, pz = prow[0:1, :], prow[1:2, :], prow[2:3, :]

    def chunk_step(i, carry):
        base = pl.multiple_of(i * CHUNK, CHUNK)

        def k_rows(j, carry):
            at = pl.multiple_of(j * 16, 16)
            q = qcol[pl.ds(base + at, 16), :]
            dx = q[:, 0:1] - px
            dy = q[:, 1:2] - py
            dz = q[:, 2:3] - pz
            sq = dx * dx + dy * dy + dz * dz + SOFTEN
            inv = lax.rsqrt(sq)
            c, s = circle(sq * inv * TURNS)
            k_sc[pl.ds(at, 16), :] = (c * inv).astype(bf16)
            k_sc[pl.ds(CHUNK + at, 16), :] = (s * inv).astype(bf16)
            return carry

        lax.fori_loop(0, CHUNK // 16, k_rows, 0)

        @pl.when(i < HALF // CHUNK)
        def _():
            c_ref[pl.ds(base, CHUNK), :] = k_sc[0:CHUNK, :]
            s_ref[pl.ds(base, CHUNK), :] = k_sc[CHUNK : 2 * CHUNK, :]

        q = qrow[:, pl.ds(base, CHUNK)]
        qx, qy, qz, qw = q[0:1], q[1:2], q[2:3], q[3:4]

        def e_rows(j, carry):
            at = pl.multiple_of(j * 32, 32)
            r = rcol[pl.ds(at, 32), :]
            c, s = circle(r[:, 0:1] * qx + r[:, 1:2] * qy + r[:, 2:3] * qz)
            c = c * qw
            s = s * qw
            cb = c.astype(bf16)
            sb = s.astype(bf16)
            e_sc[pl.ds(at, 32), 0:CHUNK] = cb
            e_sc[pl.ds(at, 32), CHUNK : 2 * CHUNK] = sb
            e_sc[pl.ds(RH + at, 32), 0:CHUNK] = sb
            e_sc[pl.ds(RH + at, 32), CHUNK : 2 * CHUNK] = -cb
            return carry

        lax.fori_loop(0, RH // 32, e_rows, 0)
        part = jnp.dot(e_sc[...], k_sc[...], preferred_element_type=f32)

        @pl.when(i == 0)
        def _():
            acc[...] = part

        @pl.when(i > 0)
        def _():
            acc[...] += part

        return carry

    lax.fori_loop(0, QS // CHUNK, chunk_step, 0)
    for g in range(NXC):
        b_ref[g, 0:RSUB, :] = acc[g * RSUB : (g + 1) * RSUB, :].astype(bf16)
        b_ref[g, RSUB : 2 * RSUB, :] = acc[RH + g * RSUB : RH + (g + 1) * RSUB, :].astype(bf16)


def vmem(count):
    return [pl.BlockSpec(memory_space=pltpu.VMEM)] * count


def tile(qrow, qcol, prow, rcol):
    return pl.pallas_call(
        tile_body,
        out_shape=[
            jax.ShapeDtypeStruct((HALF, BLOCK), bf16),
            jax.ShapeDtypeStruct((HALF, BLOCK), bf16),
            jax.ShapeDtypeStruct((NXC, 2 * RSUB, BLOCK), bf16),
        ],
        in_specs=vmem(4),
        out_specs=vmem(3),
        scratch_shapes=[
            pltpu.VMEM((2 * RH, 2 * CHUNK), bf16),
            pltpu.VMEM((2 * CHUNK, BLOCK), bf16),
            pltpu.VMEM((2 * RH, BLOCK), f32),
        ],
        cost_estimate=pl.CostEstimate(
            flops=20_000_000_000, transcendentals=QS * (BLOCK + RH) * 2, bytes_accessed=8_000_000
        ),
        name="tile",
    )(qrow, qcol, prow, rcol)


def halves(msg):
    real = msg[:, 0:JD, :].reshape(NDIR, BLOCK)
    imag = msg[:, JD : 2 * JD, :].reshape(NDIR, BLOCK)
    return real, imag


def image_body(c_ref, s_ref, msg, u_ref):
    vr, vi = halves(msg)
    c = c_ref[...]
    s = s_ref[...]
    u_ref[:, 0:NDIR] = (nt(c, vr) - nt(s, vi)).astype(bf16)
    u_ref[:, NDIR : 2 * NDIR] = (nt(s, vr) + nt(c, vi)).astype(bf16)


def image(c_own, s_own, msg):
    return pl.pallas_call(
        image_body,
        out_shape=jax.ShapeDtypeStruct((HALF, 2 * NDIR), bf16),
        in_specs=vmem(3),
        out_specs=vmem(1)[0],
        cost_estimate=pl.CostEstimate(
            flops=8 * HALF * BLOCK * NDIR, transcendentals=0, bytes_accessed=4_000_000
        ),
        name="image",
    )(c_own, s_own, msg)


def far_body(pieces, msg, direct, b_ref, f_ref):
    total = pieces[0].astype(f32)
    for g in range(1, NXC):
        total = total + pieces[g].astype(f32)
    b_ref[...] = total
    vr, vi = halves(msg)
    br = total[0:RSUB].astype(bf16)
    bi = total[RSUB : 2 * RSUB].astype(bf16)
    f_ref[:, 0:NDIR] = (direct[:, 0:NDIR] - nt(br, vr) - nt(bi, vi)).astype(bf16)
    f_ref[:, NDIR : 2 * NDIR] = (direct[:, NDIR : 2 * NDIR] - nt(br, vi) + nt(bi, vr)).astype(bf16)


def far(pieces, msg, direct):
    return pl.pallas_call(
        far_body,
        out_shape=[
            jax.ShapeDtypeStruct((2 * RSUB, BLOCK), f32),
            jax.ShapeDtypeStruct((RSUB, 2 * NDIR), bf16),
        ],
        in_specs=vmem(3),
        out_specs=vmem(2),
        name="far",
    )(pieces, msg, direct)


def grad_body(res, b_ref, msg, wz, g_ref):
    vr, vi = halves(msg)
    rr = res[:, 0:NDIR]
    ri = res[:, NDIR : 2 * NDIR]
    dot = lambda a, b: jnp.dot(a, b, preferred_element_type=f32)
    even = dot(rr, vr) + dot(ri, vi)
    odd = dot(rr, vi) - dot(ri, vr)
    terms = b_ref[0:RSUB, :] * even + b_ref[RSUB : 2 * RSUB, :] * odd
    g_ref[...] = -jnp.sum(terms, axis=0, keepdims=True) / wz[...]


def grad(res, b, msg, wz):
    return pl.pallas_call(
        grad_body,
        out_shape=jax.ShapeDtypeStruct((1, BLOCK), f32),
        in_specs=vmem(4),
        out_specs=vmem(1)[0],
        name="grad",
    )(res, b, msg, wz)


def three_parts(x):
    hi = lax.reduce_precision(x, 8, 7)
    mid = lax.reduce_precision(x - hi, 8, 7)
    low = lax.reduce_precision(x - hi - mid, 8, 7)
    return jnp.stack([hi, mid, low])


def on_device(panel_angles, impedance, quad_count, receivers, farfield_data, warm_density):
    d = lax.axis_index("dir")
    e = lax.axis_index("elem")
    zh = (d // 2) % 2
    mate = d + 2 - 4 * zh

    pos = positions(panel_angles)
    w = weights(quad_count)
    geom = jnp.concatenate([pos, w[None]], axis=0)
    part = jnp.concatenate(
        [
            lax.dynamic_slice_in_dim(geom, d * SUB, SUB, 1),
            lax.dynamic_slice_in_dim(geom, mate * SUB, SUB, 1),
        ],
        axis=1,
    )
    whole = exchange(spread(part, NE), "elem").reshape(NE, 4, 2, SUB)
    qrow = whole.transpose(1, 2, 0, 3).reshape(4, QS)
    qcol = whole.transpose(2, 0, 3, 1).reshape(QS, 4)

    order = receivers.reshape(ND, 2, NE).transpose(0, 2, 1).reshape(ND * RSUB)
    rdir = lattice(order, RBANK).reshape(3, ND, RSUB)
    half = lax.dynamic_index_in_dim(rdir.reshape(3, 4, 2, 2, RSUB), zh, 2, keepdims=False)
    rcol = (TURNS * half.reshape(3, RH)).T
    rown = lax.dynamic_index_in_dim(rdir, d, 1, keepdims=False)

    wz = w * impedance
    v = (wz * warm_density).astype(bf16).reshape(2 * JD, BLOCK)
    parts = three_parts(farfield_data.reshape(2 * JD, 2 * RH)).reshape(3 * 2 * JD, 2 * RH)
    column = lax.broadcasted_iota(jnp.int32, (2 * ND, 2 * RH), 1)
    pick = (column == NE * lax.broadcasted_iota(jnp.int32, (2 * ND, 2 * RH), 0) + e).astype(bf16)
    mine = nt(pick, parts.astype(bf16)).astype(bf16)
    rows = jnp.pad(mine.reshape(ND, 2, 6 * JD), ((0, 0), (0, 0), (0, BLOCK - 6 * JD)))
    send = jnp.concatenate([spread(v, ND), rows], axis=1)
    send, qrow, qcol = lax.optimization_barrier((send, qrow, qcol))
    msg = exchange(send, "dir")
    data = msg[:, 2 * JD :, : 6 * JD].astype(f32).reshape(ND, 2, 3, 2, JD).sum(axis=2)
    data = data.transpose(1, 2, 0, 3).reshape(2, 2 * NDIR)

    dvec = lattice(jnp.arange(NDIR, dtype=jnp.int32), NDIR)
    turns = TURNS * jnp.sum(dvec[:, :, None] * pos[:, None, :], axis=0)
    fc, fs = circle(turns)
    sc = (w * fc).astype(bf16)
    ss = (w * fs).astype(bf16)
    ec, es = circle(TURNS * jnp.sum(rown[:, :, None] * pos[:, None, :], axis=0))
    ec = ec.astype(bf16)
    es = es.astype(bf16)
    direct = jnp.concatenate([nt(ec, sc) + nt(es, ss), nt(ec, ss) - nt(es, sc)], axis=1)

    c_own, s_own, pieces = tile(qrow, qcol, pos, rcol)
    pieces = exchange(pieces, "dir", XC)
    u = image(c_own, s_own, msg)
    b, far_part = far(pieces, msg, direct)
    joined = jnp.concatenate(
        [u.reshape(NE, SUB, 2 * NDIR), far_part.reshape(NE, 2, 2 * NDIR)], axis=1
    )
    joined = exchange(joined, "elem")
    total = jnp.sum(joined[:, SUB:].astype(f32), axis=0)
    res = (total - data).astype(bf16)
    res = exchange(spread(res, NE), "elem").reshape(RSUB, 2 * NDIR)
    u_sum = jnp.sum(joined[:, :SUB].astype(f32), axis=0)
    u_out = u_sum.reshape(SUB, 2, ND, JD).transpose(2, 0, 1, 3).reshape(ND, SUB * 2 * JD)
    g_part = grad(res, b, msg, wz[None])
    last = jnp.concatenate([u_out, jnp.broadcast_to(g_part, (ND, BLOCK))], axis=1)
    last = exchange(last, "dir")
    gradient = jnp.sum(last[:, SUB * 2 * JD :], axis=0) / NDIR
    u_in = last[:, : SUB * 2 * JD].reshape(ND, SUB, 2, JD).transpose(2, 3, 0, 1).reshape(2, JD, BLOCK)
    own = lattice(d * JD + jnp.arange(JD, dtype=jnp.int32), NDIR)
    oc, os = circle(TURNS * jnp.sum(own[:, :, None] * pos[:, None, :], axis=0))
    return gradient, jnp.stack([oc, os]) - u_in


def solution(mesh):
    placed = (
        P(None, "elem"),
        P("elem"),
        P("elem"),
        P(),
        P(None, "dir", None),
        P(None, "dir", "elem"),
    )
    return jax.shard_map(
        on_device,
        mesh=mesh,
        in_specs=placed,
        out_specs=(P("elem"), P(None, "dir", "elem")),
        check_vma=False,
    )
```

```python
import math

import jax
import jax.numpy as jnp
from jax import lax
from jax.experimental import pallas as pl
from jax.experimental.pallas import tpu as pltpu
from jax.sharding import PartitionSpec as P

PANELS = 16384
RBANK = 4096
NDIR = 256
WAVENUM = 32.0
SOFTEN = 0.0025
TURNS = WAVENUM / (2.0 * math.pi)

ND = 16
NE = 32
BLOCK = PANELS // NE
SUB = BLOCK // ND
RSUB = 1024 // ND
JD = NDIR // ND
HALF = NE * SUB
QS = 2 * HALF
RH = 1024 // 2
CHUNK = 256
PARTS = 4
LT = BLOCK // 128
NXC = 8
XC = [[x * 4 + zh * 2 + c for x in range(4) for c in range(2)] for zh in range(2)]

SIN = (6.28318492, -41.34158923, 81.59994333, -76.61447253, 41.34288235, -12.47124353)
COS = (0.99999999, -19.7392045, 64.93911746, -85.45013953, 60.16763095, -25.96759925, 6.52865816)

bf16 = jnp.bfloat16
f32 = jnp.float32


def horner(coef, z):
    acc = coef[-1] * z + coef[-2]
    for c in coef[-3::-1]:
        acc = acc * z + c
    return acc


def circle(turns):
    r = turns - jnp.round(turns)
    z = r * r
    return horner(COS, z), r * horner(SIN, z)


def exchange(x, axis, groups=None):
    return lax.all_to_all(x, axis, 0, 0, axis_index_groups=groups, tiled=True)


def spread(x, count):
    return jnp.broadcast_to(x[None], (count, *x.shape))


def positions(angles):
    phi = angles[0]
    psi = angles[1]
    return jnp.stack(
        [4.0 * jnp.cos(psi), jnp.sin(psi) * jnp.cos(phi), 0.6 * jnp.sin(psi) * jnp.sin(phi)]
    )


def weights(counts):
    return counts.astype(f32) * (0.5 / (4.0 * math.sqrt(PANELS)))


def lattice(index, count):
    where = index.astype(f32)
    height = 1.0 - (2.0 * where + 1.0) / count
    radius = jnp.sqrt(1.0 - height * height)
    turn = where * (math.pi * (3.0 - math.sqrt(5.0)))
    return jnp.stack([radius * jnp.cos(turn), radius * jnp.sin(turn), height])


def nt(a, b):
    return lax.dot_general(a, b, (((1,), (1,)), ((), ())), preferred_element_type=f32)


def tile_body(qrow, qcol, prow, rcol, c_ref, s_ref, b_ref, e0, e1, k0, k1, acc):
    px, py, pz = prow[0:1, :], prow[1:2, :], prow[2:3, :]
    tables = ((e0, k0), (e1, k1))
    stages = QS // CHUNK

    def build(stage, j):
        e_sc, k_sc = tables[stage % 2]
        base = stage * CHUNK
        for n in range(CHUNK // PARTS // 16):
            at = pl.multiple_of(j * (CHUNK // PARTS) + n * 16, 16)
            q = qcol[pl.ds(base + at, 16), :]
            dx = q[:, 0:1] - px
            dy = q[:, 1:2] - py
            dz = q[:, 2:3] - pz
            sq = dx * dx + dy * dy + dz * dz + SOFTEN
            inv = lax.rsqrt(sq)
            c, s = circle(sq * inv * TURNS)
            c = (c * inv).astype(bf16)
            s = (s * inv).astype(bf16)
            k_sc[pl.ds(at, 16), :] = c
            k_sc[pl.ds(CHUNK + at, 16), :] = s
            if base < HALF:
                c_ref[pl.ds(base + at, 16), :] = c
                s_ref[pl.ds(base + at, 16), :] = s
        q = qrow[:, base : base + CHUNK]
        qx, qy, qz, qw = q[0:1], q[1:2], q[2:3], q[3:4]
        for n in range(RH // PARTS // 32):
            at = pl.multiple_of(j * (RH // PARTS) + n * 32, 32)
            r = rcol[pl.ds(at, 32), :]
            c, s = circle(r[:, 0:1] * qx + r[:, 1:2] * qy + r[:, 2:3] * qz)
            c = (c * qw).astype(bf16)
            s = (s * qw).astype(bf16)
            e_sc[pl.ds(at, 32), 0:CHUNK] = c
            e_sc[pl.ds(at, 32), CHUNK : 2 * CHUNK] = s
            e_sc[pl.ds(RH + at, 32), 0:CHUNK] = s
            e_sc[pl.ds(RH + at, 32), CHUNK : 2 * CHUNK] = -c

    rows = 2 * RH // PARTS

    def product(stage, j):
        e_sc, k_sc = tables[stage % 2]
        at = pl.multiple_of(j * rows, rows)
        part = jnp.dot(e_sc[pl.ds(at, rows), :], k_sc[...], preferred_element_type=f32)
        if stage > 0:
            part = part + acc[pl.ds(at, rows), :]
        return at, part

    for stage in range(stages):

        def step(j, carry, stage=stage):
            if stage > 0:
                at, part = product(stage - 1, j)
                acc[pl.ds(at, rows), :] = part
            build(stage, j)
            return carry

        lax.fori_loop(0, PARTS, step, 0)
    for j in range(PARTS):
        _, part = product(stages - 1, j)
        for n in range(rows // RSUB):
            first = j * rows + n * RSUB
            b_ref[(first % RH) // RSUB, pl.ds((first // RH) * RSUB, RSUB), :] = part[
                n * RSUB : (n + 1) * RSUB, :
            ].astype(bf16)


def vmem(count):
    return [pl.BlockSpec(memory_space=pltpu.VMEM)] * count


def room(mib):
    return pltpu.CompilerParams(vmem_limit_bytes=mib << 20)


def tile(qrow, qcol, prow, rcol):
    return pl.pallas_call(
        tile_body,
        out_shape=[
            jax.ShapeDtypeStruct((HALF, BLOCK), bf16),
            jax.ShapeDtypeStruct((HALF, BLOCK), bf16),
            jax.ShapeDtypeStruct((NXC, 2 * RSUB, BLOCK), bf16),
        ],
        in_specs=vmem(4),
        out_specs=vmem(3),
        scratch_shapes=[
            pltpu.VMEM((2 * RH, 2 * CHUNK), bf16),
            pltpu.VMEM((2 * RH, 2 * CHUNK), bf16),
            pltpu.VMEM((2 * CHUNK, BLOCK), bf16),
            pltpu.VMEM((2 * CHUNK, BLOCK), bf16),
            pltpu.VMEM((2 * RH, BLOCK), f32),
        ],
        compiler_params=room(32),
        cost_estimate=pl.CostEstimate(
            flops=20_000_000_000, transcendentals=QS * (BLOCK + RH) * 2, bytes_accessed=8_000_000
        ),
        name="tile",
    )(qrow, qcol, prow, rcol)


def image_body(c_ref, s_ref, msg, v_ref, u_ref):
    for n in range(ND):
        for t in range(LT):
            for ri in range(2):
                v_ref[ri, n * JD : (n + 1) * JD, t * 128 : (t + 1) * 128] = msg[
                    n, t * 2 * JD + ri * JD : t * 2 * JD + (ri + 1) * JD, :
                ]
    vr = v_ref[0]
    vi = v_ref[1]
    c = c_ref[...]
    s = s_ref[...]
    real = (nt(c, vr) - nt(s, vi)).astype(bf16)
    imag = (nt(s, vr) + nt(c, vi)).astype(bf16)
    for n in range(NE):
        for t in range(LT):
            source = (real, imag)[t // 2]
            u_ref[n, t * SUB : (t + 1) * SUB, :] = source[
                n * SUB : (n + 1) * SUB, (t % 2) * 128 : (t % 2 + 1) * 128
            ]


def image(c_own, s_own, msg):
    return pl.pallas_call(
        image_body,
        out_shape=[
            jax.ShapeDtypeStruct((2, NDIR, BLOCK), bf16),
            jax.ShapeDtypeStruct((NE, LT * SUB, 128), bf16),
        ],
        in_specs=vmem(3),
        out_specs=vmem(2),
        compiler_params=room(24),
        cost_estimate=pl.CostEstimate(
            flops=8 * HALF * BLOCK * NDIR, transcendentals=0, bytes_accessed=4_000_000
        ),
        name="image",
    )(c_own, s_own, msg)


def far_body(pieces, v_ref, direct, b_ref, f_ref):
    total = pieces[0].astype(f32)
    for g in range(1, NXC):
        total = total + pieces[g].astype(f32)
    b_ref[...] = total
    vr = v_ref[0]
    vi = v_ref[1]
    br = total[0:RSUB].astype(bf16)
    bi = total[RSUB : 2 * RSUB].astype(bf16)
    real = direct[:, 0:NDIR] - nt(br, vr) - nt(bi, vi)
    imag = direct[:, NDIR : 2 * NDIR] - nt(br, vi) + nt(bi, vr)
    for n in range(NE):
        t = n % LT
        at = (n // LT) * 8
        source = (real, imag)[t // 2]
        f_ref[n] = source[at : at + 8, (t % 2) * 128 : (t % 2 + 1) * 128].astype(bf16)


def far(pieces, v, direct):
    return pl.pallas_call(
        far_body,
        out_shape=[
            jax.ShapeDtypeStruct((2 * RSUB, BLOCK), f32),
            jax.ShapeDtypeStruct((NE, 8, 128), bf16),
        ],
        in_specs=vmem(3),
        out_specs=vmem(2),
        compiler_params=room(16),
        name="far",
    )(pieces, v, direct)


def grad_body(res_ref, b_ref, v_ref, wz, g_ref):
    vr = v_ref[0]
    vi = v_ref[1]
    res = jnp.concatenate(
        [
            jnp.concatenate([res_ref[m * LT + t].astype(f32) for t in range(LT)], axis=1)
            for m in range(NE // LT)
        ],
        axis=0,
    ).astype(bf16)
    rr = res[:, 0:NDIR]
    ri = res[:, NDIR : 2 * NDIR]
    dot = lambda a, b: jnp.dot(a, b, preferred_element_type=f32)
    even = dot(rr, vr) + dot(ri, vi)
    odd = dot(rr, vi) - dot(ri, vr)
    terms = b_ref[0:RSUB, :] * even + b_ref[RSUB : 2 * RSUB, :] * odd
    g_ref[...] = -jnp.sum(terms, axis=0, keepdims=True) / wz[...]


def grad(res, b, v, wz):
    return pl.pallas_call(
        grad_body,
        out_shape=jax.ShapeDtypeStruct((1, BLOCK), f32),
        in_specs=vmem(4),
        out_specs=vmem(1)[0],
        compiler_params=room(16),
        name="grad",
    )(res, b, v, wz)


def three_parts(x):
    hi = lax.reduce_precision(x, 8, 7)
    mid = lax.reduce_precision(x - hi, 8, 7)
    low = lax.reduce_precision(x - hi - mid, 8, 7)
    return jnp.stack([hi, mid, low])


def on_device(panel_angles, impedance, quad_count, receivers, farfield_data, warm_density):
    d = lax.axis_index("dir")
    e = lax.axis_index("elem")
    zh = (d // 2) % 2
    mate = d + 2 - 4 * zh

    pos = positions(panel_angles)
    w = weights(quad_count)
    geom = jnp.concatenate([pos, w[None]], axis=0)
    part = jnp.concatenate(
        [
            lax.dynamic_slice_in_dim(geom, d * SUB, SUB, 1),
            lax.dynamic_slice_in_dim(geom, mate * SUB, SUB, 1),
        ],
        axis=1,
    )
    whole = exchange(spread(part, NE), "elem").reshape(NE, 4, 2, SUB)
    qrow = whole.transpose(1, 2, 0, 3).reshape(4, QS)
    qcol = whole.transpose(2, 0, 3, 1).reshape(QS, 4)

    rdir = lattice(receivers, RBANK).reshape(3, ND, RSUB)
    half = lax.dynamic_index_in_dim(rdir.reshape(3, 4, 2, 2, RSUB), zh, 2, keepdims=False)
    rcol = (TURNS * half.reshape(3, RH)).T
    rown = lax.dynamic_index_in_dim(rdir, d, 1, keepdims=False)

    octet = e // LT
    lane = e % LT
    wz = w * impedance
    v = (wz * warm_density).astype(bf16).reshape(2 * JD, LT, 128).transpose(1, 0, 2)
    v = v.reshape(LT * 2 * JD, 128)
    given = lax.dynamic_index_in_dim(farfield_data, lane // 2, 0, keepdims=False)
    parts = three_parts(given).reshape(3 * JD, 2 * RH).astype(bf16)
    column = lax.broadcasted_iota(jnp.int32, (128, 2 * RH), 1)
    line = lax.broadcasted_iota(jnp.int32, (128, 2 * RH), 0)
    pick = (column == (line // 8) * RSUB + 8 * octet + line % 8).astype(bf16)
    mine = nt(pick, parts).astype(bf16).reshape(ND, 8, 3, JD).transpose(0, 2, 1, 3)
    rows = jnp.pad(mine.reshape(ND, 3, 128), ((0, 0), (0, 5), (0, 0)))
    send = jnp.concatenate([spread(v, ND), rows], axis=1)
    send, qrow, qcol = lax.optimization_barrier((send, qrow, qcol))
    msg = exchange(send, "dir")
    data = msg[:, LT * 2 * JD : LT * 2 * JD + 3].astype(f32).sum(axis=1)
    data = lax.dynamic_slice_in_dim(data, (lane % 2) * 8, 8, 0)
    data = data.reshape(8, 8, JD).transpose(1, 0, 2).reshape(8, 128)

    dvec = lattice(jnp.arange(NDIR, dtype=jnp.int32), NDIR)
    turns = TURNS * jnp.sum(dvec[:, :, None] * pos[:, None, :], axis=0)
    fc, fs = circle(turns)
    sc = (w * fc).astype(bf16)
    ss = (w * fs).astype(bf16)
    ec, es = circle(TURNS * jnp.sum(rown[:, :, None] * pos[:, None, :], axis=0))
    ec = ec.astype(bf16)
    es = es.astype(bf16)
    direct = jnp.concatenate([nt(ec, sc) + nt(es, ss), nt(ec, ss) - nt(es, sc)], axis=1)

    c_own, s_own, pieces = tile(qrow, qcol, pos, rcol)
    pieces, msg = lax.optimization_barrier((pieces, msg))
    pieces = exchange(pieces, "dir", XC)
    v, u = image(c_own, s_own, msg)
    b, far_part = far(pieces, v, direct)
    joined = exchange(jnp.concatenate([u, far_part], axis=1), "elem")
    total = jnp.sum(joined[:, LT * SUB :].astype(f32), axis=0)
    res = exchange(spread((total - data).astype(bf16), NE), "elem")
    u_sum = jnp.sum(joined[:, : LT * SUB].astype(f32), axis=0)
    u_out = u_sum.reshape(2, 2, SUB, 8, JD).transpose(1, 3, 2, 0, 4).reshape(ND, SUB * 2 * JD)
    g_part = grad(res, b, v, wz[None])
    last = jnp.concatenate([u_out, jnp.broadcast_to(g_part, (ND, BLOCK))], axis=1)
    last = exchange(last, "dir")
    gradient = jnp.sum(last[:, SUB * 2 * JD :], axis=0) / NDIR
    u_in = last[:, : SUB * 2 * JD].reshape(ND, SUB, 2, JD).transpose(2, 3, 0, 1).reshape(2, JD, BLOCK)
    own = lattice(d * JD + jnp.arange(JD, dtype=jnp.int32), NDIR)
    oc, os = circle(TURNS * jnp.sum(own[:, :, None] * pos[:, None, :], axis=0))
    return gradient, jnp.stack([oc, os]) - u_in


def solution(mesh):
    placed = (
        P(None, "elem"),
        P("elem"),
        P("elem"),
        P(),
        P(None, "dir", None),
        P(None, "dir", "elem"),
    )
    return jax.shard_map(
        on_device,
        mesh=mesh,
        in_specs=placed,
        out_specs=(P("elem"), P(None, "dir", "elem")),
        check_vma=False,
    )
```

```python
import math

import jax
import jax.numpy as jnp
from jax import lax
from jax.experimental import pallas as pl
from jax.experimental.pallas import tpu as pltpu
from jax.sharding import PartitionSpec as P


PANELS = 16384
RBANK = 4096
NDIR = 256
WAVENUM = 32.0
SOFTEN = 0.0025
TURNS = WAVENUM / (2.0 * math.pi)

ND = 16
NE = 32
BLOCK = PANELS // NE
SUB = BLOCK // ND
RSUB = 1024 // ND
JD = NDIR // ND
HALF = NE * SUB
QS = 2 * HALF
RH = 1024 // 2
CHUNK = 256
PARTS = 4
LT = BLOCK // 128
NXC = 8
NZ = 4
NY = 8
XC = [[x * 4 + zh * 2 + c for x in range(4) for c in range(2)] for zh in range(2)]

SIN = (6.28318492, -41.34158923, 81.59994333, -76.61447253, 41.34288235, -12.47124353)
COS = (0.99999999, -19.7392045, 64.93911746, -85.45013953, 60.16763095, -25.96759925, 6.52865816)

bf16 = jnp.bfloat16
f32 = jnp.float32


def horner(coef, z):
    acc = coef[-1] * z + coef[-2]
    for c in coef[-3::-1]:
        acc = acc * z + c
    return acc


def circle(turns):
    r = turns - jnp.round(turns)
    z = r * r
    return horner(COS, z), r * horner(SIN, z)


def exchange(x, axis, groups=None):
    return lax.all_to_all(x, axis, 0, 0, axis_index_groups=groups, tiled=True)


def spread(x, count):
    return jnp.broadcast_to(x[None], (count, *x.shape))


def positions(angles):
    phi = angles[0]
    psi = angles[1]
    return jnp.stack(
        [4.0 * jnp.cos(psi), jnp.sin(psi) * jnp.cos(phi), 0.6 * jnp.sin(psi) * jnp.sin(phi)]
    )


def weights(counts):
    return counts.astype(f32) * (0.5 / (4.0 * math.sqrt(PANELS)))


def lattice(index, count):
    where = index.astype(f32)
    height = 1.0 - (2.0 * where + 1.0) / count
    radius = jnp.sqrt(1.0 - height * height)
    turn = where * (math.pi * (3.0 - math.sqrt(5.0)))
    return jnp.stack([radius * jnp.cos(turn), radius * jnp.sin(turn), height])


def nt(a, b):
    return lax.dot_general(a, b, (((1,), (1,)), ((), ())), preferred_element_type=f32)


def tile_body(qrow, qcol, prow, rcol, c_ref, s_ref, b_ref, e0, e1, k0, k1, acc):
    px, py, pz = prow[0:1, :], prow[1:2, :], prow[2:3, :]
    tables = ((e0, k0), (e1, k1))
    stages = QS // CHUNK

    def build(stage, j):
        e_sc, k_sc = tables[stage % 2]
        base = stage * CHUNK
        for n in range(CHUNK // PARTS // 16):
            at = pl.multiple_of(j * (CHUNK // PARTS) + n * 16, 16)
            q = qcol[pl.ds(base + at, 16), :]
            dx = q[:, 0:1] - px
            dy = q[:, 1:2] - py
            dz = q[:, 2:3] - pz
            sq = dx * dx + dy * dy + dz * dz + SOFTEN
            inv = lax.rsqrt(sq)
            c, s = circle(sq * inv * TURNS)
            c = (c * inv).astype(bf16)
            s = (s * inv).astype(bf16)
            k_sc[pl.ds(at, 16), :] = c
            k_sc[pl.ds(CHUNK + at, 16), :] = s
            if base < HALF:
                c_ref[pl.ds(base + at, 16), :] = c
                s_ref[pl.ds(base + at, 16), :] = s
        q = qrow[:, base : base + CHUNK]
        qx, qy, qz, qw = q[0:1], q[1:2], q[2:3], q[3:4]
        for n in range(RH // PARTS // 32):
            at = pl.multiple_of(j * (RH // PARTS) + n * 32, 32)
            r = rcol[pl.ds(at, 32), :]
            c, s = circle(r[:, 0:1] * qx + r[:, 1:2] * qy + r[:, 2:3] * qz)
            c = (c * qw).astype(bf16)
            s = (s * qw).astype(bf16)
            e_sc[pl.ds(at, 32), 0:CHUNK] = c
            e_sc[pl.ds(at, 32), CHUNK : 2 * CHUNK] = s
            e_sc[pl.ds(RH + at, 32), 0:CHUNK] = s
            e_sc[pl.ds(RH + at, 32), CHUNK : 2 * CHUNK] = -c

    rows = 2 * RH // PARTS

    def product(stage, j):
        e_sc, k_sc = tables[stage % 2]
        at = pl.multiple_of(j * rows, rows)
        part = jnp.dot(e_sc[pl.ds(at, rows), :], k_sc[...], preferred_element_type=f32)
        if stage > 0:
            part = part + acc[pl.ds(at, rows), :]
        return at, part

    for stage in range(stages):

        def step(j, carry, stage=stage):
            if stage > 0:
                at, part = product(stage - 1, j)
                acc[pl.ds(at, rows), :] = part
            build(stage, j)
            return carry

        lax.fori_loop(0, PARTS, step, 0)
    for j in range(PARTS):
        _, part = product(stages - 1, j)
        for n in range(rows // RSUB):
            first = j * rows + n * RSUB
            b_ref[(first % RH) // RSUB, pl.ds((first // RH) * RSUB, RSUB), :] = part[
                n * RSUB : (n + 1) * RSUB, :
            ].astype(bf16)


def vmem(count):
    return [pl.BlockSpec(memory_space=pltpu.VMEM)] * count


def room(mib):
    return pltpu.CompilerParams(vmem_limit_bytes=mib << 20)


def tile(qrow, qcol, prow, rcol):
    return pl.pallas_call(
        tile_body,
        out_shape=[
            jax.ShapeDtypeStruct((HALF, BLOCK), bf16),
            jax.ShapeDtypeStruct((HALF, BLOCK), bf16),
            jax.ShapeDtypeStruct((NXC, 2 * RSUB, BLOCK), bf16),
        ],
        in_specs=vmem(4),
        out_specs=vmem(3),
        scratch_shapes=[
            pltpu.VMEM((2 * RH, 2 * CHUNK), bf16),
            pltpu.VMEM((2 * RH, 2 * CHUNK), bf16),
            pltpu.VMEM((2 * CHUNK, BLOCK), bf16),
            pltpu.VMEM((2 * CHUNK, BLOCK), bf16),
            pltpu.VMEM((2 * RH, BLOCK), f32),
        ],
        compiler_params=room(32),
        cost_estimate=pl.CostEstimate(
            flops=20_000_000_000, transcendentals=QS * (BLOCK + RH) * 2, bytes_accessed=8_000_000
        ),
        name="tile",
    )(qrow, qcol, prow, rcol)


def image_body(place, c_ref, s_ref, msg, v_ref, *u_refs):
    for n in range(ND):
        for t in range(LT):
            for ri in range(2):
                v_ref[ri, n * JD : (n + 1) * JD, t * 128 : (t + 1) * 128] = msg[
                    n, t * 2 * JD + ri * JD : t * 2 * JD + (ri + 1) * JD, :
                ]
    vr = v_ref[0]
    vi = v_ref[1]
    y = place[1]
    for k in range(NY):
        to = lax.rem(y + k, NY)
        rows = [pl.ds(pl.multiple_of((z * NY + to) * SUB, SUB), SUB) for z in range(NZ)]
        c = jnp.concatenate([c_ref[r, :] for r in rows], axis=0)
        s = jnp.concatenate([s_ref[r, :] for r in rows], axis=0)
        real = (nt(c, vr) - nt(s, vi)).astype(bf16)
        imag = (nt(s, vr) + nt(c, vi)).astype(bf16)
        for z in range(NZ):
            for t in range(LT):
                source = (real, imag)[t // 2]
                u_refs[k][z, t * SUB : (t + 1) * SUB, :] = source[
                    z * SUB : (z + 1) * SUB, (t % 2) * 128 : (t % 2 + 1) * 128
                ]


def image(place, c_own, s_own, msg):
    return pl.pallas_call(
        image_body,
        out_shape=[jax.ShapeDtypeStruct((2, NDIR, BLOCK), bf16)]
        + [jax.ShapeDtypeStruct((NZ, LT * SUB, 128), bf16)] * NY,
        in_specs=[pl.BlockSpec(memory_space=pltpu.SMEM)] + vmem(3),
        out_specs=vmem(1 + NY),
        compiler_params=room(24),
        cost_estimate=pl.CostEstimate(
            flops=8 * HALF * BLOCK * NDIR, transcendentals=0, bytes_accessed=4_000_000
        ),
        name="image",
    )(place, c_own, s_own, msg)


def line_body(place, *refs):
    parts, outs = refs[:NY], refs[NY:]
    z = place[0]
    for k in range(NZ):
        to = lax.rem(z + k, NZ)
        total = parts[0][to].astype(f32)
        for part in parts[1:]:
            total = total + part[to].astype(f32)
        outs[k][...] = total.astype(bf16)


def line_sums(place, parts):
    return pl.pallas_call(
        line_body,
        out_shape=[jax.ShapeDtypeStruct((LT * SUB, 128), bf16)] * NZ,
        in_specs=[pl.BlockSpec(memory_space=pltpu.SMEM)] + vmem(NY),
        out_specs=vmem(NZ),
        compiler_params=room(8),
        name="line",
    )(place, *parts)


def shift_y(x, k):
    return lax.ppermute(
        x, "elem", [(z * NY + y, z * NY + (y + k) % NY) for z in range(NZ) for y in range(NY)]
    )


def shift_z(x, k):
    return lax.ppermute(
        x, "elem", [(z * NY + y, (z + k) % NZ * NY + y) for z in range(NZ) for y in range(NY)]
    )


def far_body(pieces, v_ref, direct, b_ref, f_ref):
    total = pieces[0].astype(f32)
    for g in range(1, NXC):
        total = total + pieces[g].astype(f32)
    b_ref[...] = total
    vr = v_ref[0]
    vi = v_ref[1]
    br = total[0:RSUB].astype(bf16)
    bi = total[RSUB : 2 * RSUB].astype(bf16)
    real = direct[:, 0:NDIR] - nt(br, vr) - nt(bi, vi)
    imag = direct[:, NDIR : 2 * NDIR] - nt(br, vi) + nt(bi, vr)
    for n in range(NE):
        t = n % LT
        at = (n // LT) * 8
        source = (real, imag)[t // 2]
        f_ref[n] = source[at : at + 8, (t % 2) * 128 : (t % 2 + 1) * 128].astype(bf16)


def far(pieces, v, direct):
    return pl.pallas_call(
        far_body,
        out_shape=[
            jax.ShapeDtypeStruct((2 * RSUB, BLOCK), f32),
            jax.ShapeDtypeStruct((NE, 8, 128), bf16),
        ],
        in_specs=vmem(3),
        out_specs=vmem(2),
        compiler_params=room(16),
        name="far",
    )(pieces, v, direct)


def grad_body(res_ref, b_ref, v_ref, wz, g_ref):
    vr = v_ref[0]
    vi = v_ref[1]
    res = jnp.concatenate(
        [
            jnp.concatenate([res_ref[m * LT + t].astype(f32) for t in range(LT)], axis=1)
            for m in range(NE // LT)
        ],
        axis=0,
    ).astype(bf16)
    rr = res[:, 0:NDIR]
    ri = res[:, NDIR : 2 * NDIR]
    dot = lambda a, b: jnp.dot(a, b, preferred_element_type=f32)
    even = dot(rr, vr) + dot(ri, vi)
    odd = dot(rr, vi) - dot(ri, vr)
    terms = b_ref[0:RSUB, :] * even + b_ref[RSUB : 2 * RSUB, :] * odd
    g_ref[...] = -jnp.sum(terms, axis=0, keepdims=True) / wz[...]


def grad(res, b, v, wz):
    return pl.pallas_call(
        grad_body,
        out_shape=jax.ShapeDtypeStruct((1, BLOCK), f32),
        in_specs=vmem(4),
        out_specs=vmem(1)[0],
        compiler_params=room(16),
        name="grad",
    )(res, b, v, wz)


def three_parts(x):
    hi = lax.reduce_precision(x, 8, 7)
    mid = lax.reduce_precision(x - hi, 8, 7)
    low = lax.reduce_precision(x - hi - mid, 8, 7)
    return jnp.stack([hi, mid, low])


def on_device(panel_angles, impedance, quad_count, receivers, farfield_data, warm_density):
    d = lax.axis_index("dir")
    e = lax.axis_index("elem")
    zh = (d // 2) % 2
    mate = d + 2 - 4 * zh

    pos = positions(panel_angles)
    w = weights(quad_count)
    geom = jnp.concatenate([pos, w[None]], axis=0)
    part = jnp.concatenate(
        [
            lax.dynamic_slice_in_dim(geom, d * SUB, SUB, 1),
            lax.dynamic_slice_in_dim(geom, mate * SUB, SUB, 1),
        ],
        axis=1,
    )
    whole = exchange(spread(part, NE), "elem").reshape(NE, 4, 2, SUB)
    qrow = whole.transpose(1, 2, 0, 3).reshape(4, QS)
    qcol = whole.transpose(2, 0, 3, 1).reshape(QS, 4)

    rdir = lattice(receivers, RBANK).reshape(3, ND, RSUB)
    half = lax.dynamic_index_in_dim(rdir.reshape(3, 4, 2, 2, RSUB), zh, 2, keepdims=False)
    rcol = (TURNS * half.reshape(3, RH)).T
    rown = lax.dynamic_index_in_dim(rdir, d, 1, keepdims=False)

    octet = e // LT
    lane = e % LT
    wz = w * impedance
    v = (wz * warm_density).astype(bf16).reshape(2 * JD, LT, 128).transpose(1, 0, 2)
    v = v.reshape(LT * 2 * JD, 128)
    given = lax.dynamic_index_in_dim(farfield_data, lane // 2, 0, keepdims=False)
    parts = three_parts(given).reshape(3 * JD, 2 * RH).astype(bf16)
    column = lax.broadcasted_iota(jnp.int32, (128, 2 * RH), 1)
    line = lax.broadcasted_iota(jnp.int32, (128, 2 * RH), 0)
    pick = (column == (line // 8) * RSUB + 8 * octet + line % 8).astype(bf16)
    mine = nt(pick, parts).astype(bf16).reshape(ND, 8, 3, JD).transpose(0, 2, 1, 3)
    rows = jnp.pad(mine.reshape(ND, 3, 128), ((0, 0), (0, 5), (0, 0)))
    send = jnp.concatenate([spread(v, ND), rows], axis=1)
    send, qrow, qcol = lax.optimization_barrier((send, qrow, qcol))
    msg = exchange(send, "dir")
    data = msg[:, LT * 2 * JD : LT * 2 * JD + 3].astype(f32).sum(axis=1)
    data = lax.dynamic_slice_in_dim(data, (lane % 2) * 8, 8, 0)
    data = data.reshape(8, 8, JD).transpose(1, 0, 2).reshape(8, 128)

    dvec = lattice(jnp.arange(NDIR, dtype=jnp.int32), NDIR)
    turns = TURNS * jnp.sum(dvec[:, :, None] * pos[:, None, :], axis=0)
    fc, fs = circle(turns)
    sc = (w * fc).astype(bf16)
    ss = (w * fs).astype(bf16)
    ec, es = circle(TURNS * jnp.sum(rown[:, :, None] * pos[:, None, :], axis=0))
    ec = ec.astype(bf16)
    es = es.astype(bf16)
    direct = jnp.concatenate([nt(ec, sc) + nt(es, ss), nt(ec, ss) - nt(es, sc)], axis=1)

    place = jnp.stack([e // NY, e % NY]).astype(jnp.int32)
    c_own, s_own, pieces = tile(qrow, qcol, pos, rcol)
    pieces, msg = lax.optimization_barrier((pieces, msg))
    v, *u = image(place, c_own, s_own, msg)
    pieces = exchange(pieces, "dir", XC)
    for k in range(1, NY):
        u[k] = shift_y(u[k], k)
    b, far_part = far(pieces, v, direct)
    far_all = exchange(far_part, "elem")
    total = jnp.sum(far_all.astype(f32), axis=0)
    res = spread((total - data).astype(bf16), NE)
    lines = list(line_sums(place, u))
    res = exchange(res, "elem")
    for k in range(1, NZ):
        lines[k] = shift_z(lines[k], k)
    g_part = grad(res, b, v, wz[None])
    u_sum = sum(x.astype(f32) for x in lines)
    u_out = u_sum.reshape(2, 2, SUB, 8, JD).transpose(1, 3, 2, 0, 4).reshape(ND, SUB * 2 * JD)
    last = jnp.concatenate([u_out, jnp.broadcast_to(g_part, (ND, BLOCK))], axis=1)
    last = exchange(last, "dir")
    gradient = jnp.sum(last[:, SUB * 2 * JD :], axis=0) / NDIR
    u_in = last[:, : SUB * 2 * JD].reshape(ND, SUB, 2, JD).transpose(2, 3, 0, 1).reshape(2, JD, BLOCK)
    own = lattice(d * JD + jnp.arange(JD, dtype=jnp.int32), NDIR)
    oc, os = circle(TURNS * jnp.sum(own[:, :, None] * pos[:, None, :], axis=0))
    return gradient, jnp.stack([oc, os]) - u_in


def solution(mesh):
    placed = (
        P(None, "elem"),
        P("elem"),
        P("elem"),
        P(),
        P(None, "dir", None),
        P(None, "dir", "elem"),
    )
    return jax.shard_map(
        on_device,
        mesh=mesh,
        in_specs=placed,
        out_specs=(P("elem"), P(None, "dir", "elem")),
        check_vma=False,
    )
```
